512 devices in a mesh: head: 8 (over y, x_hi), seq: 16 (over z), dp: 4 (over x_lo, core).
Axes of the slice: x: 4 (x_hi: 2, x_lo: 2; x = x_hi * 2 + x_lo), y: 4, z: 16, core: 2. Of those that a mesh axis runs over, the one named last changes fastest.
Arguments:
- teacher_query: bfloat16 [4, 2048, 3072], P('dp', 'seq', 'head'), may hold values from -6 to 6
- teacher_key: bfloat16 [4, 2048, 3072], P('dp', 'seq', 'head'), may hold values from -6 to 6
- student_query: bfloat16 [4, 2048, 512], P('dp', 'seq'), may hold values from -6 to 6
- student_key: bfloat16 [4, 2048, 512], P('dp', 'seq'), may hold values from -6 to 6
- head_mix: float32 [24, 8], P('head'), may hold values from 0.02 to 0.25
Outputs:
- grad_query: float32 [4, 2048, 512], P('dp', 'seq', 'head')
- grad_key: float32 [4, 2048, 512], P('dp', 'seq', 'head')
- grad_mix: float32 [24, 8], P('head')
- head_loss: float32 [24], P('head')
The draws below stay inside these ranges and needn't reach their ends.
All inputs are finite; a program needn't handle non-finite values.
Results may differ from the reference program's by a relative error of at most 0.0012.
Values may be sent and summed in bfloat16 or wider, within the bound.
A program may use at most 64 MiB of HBM per device.

```python
import math
import jax
import jax.numpy as jnp
from jax import lax

HEADS_T = 24
HD_T = 128
HEADS_S = 8
HD_S = 64
SEQ = 2048
IMAGES = 4
N_HEAD = 8


def paired(key, width):
    extent = (IMAGES, SEQ, width)
    draw_one, draw_two = jax.random.split(key, 2)
    queries = jnp.clip(jax.random.normal(draw_one, extent, jnp.float32), -6.0, 6.0)
    key_rows = jnp.clip(jax.random.normal(draw_two, extent, jnp.float32), -6.0, 6.0)
    return (queries, key_rows)


def draw_teacher_query(key, part):
    return paired(jax.random.fold_in(key, 11), HEADS_T * HD_T)[0].astype(jnp.bfloat16)


def draw_teacher_key(key, part):
    return paired(jax.random.fold_in(key, 11), HEADS_T * HD_T)[1].astype(jnp.bfloat16)


def draw_student_query(key, part):
    return paired(jax.random.fold_in(key, 23), HEADS_S * HD_S)[0].astype(jnp.bfloat16)


def draw_student_key(key, part):
    return paired(jax.random.fold_in(key, 23), HEADS_S * HD_S)[1].astype(jnp.bfloat16)


def level_of(stream_key, dims, pieces, low, high):
    loudness, own = 1.0, jax.random.fold_in(stream_key, 6)
    for position, blocks in pieces:
        draws = jnp.exp(jax.random.uniform(jax.random.fold_in(own, position), (blocks,), jnp.float32, low / len(pieces), high / len(pieces)))
        loudness = loudness * jnp.repeat(draws, dims[position] // blocks).reshape([-1 if axis == position else 1 for axis in range(len(dims))])
    return loudness


def setup_inputs(seed: int = 0) -> dict:
    streams_of = jax.random.split(jax.random.key(seed), 6)
    teacher_query = draw_teacher_query(jax.random.fold_in(streams_of[5], 71), 0)
    teacher_key = draw_teacher_key(jax.random.fold_in(streams_of[5], 71), 0)
    student_query = draw_student_query(jax.random.fold_in(streams_of[5], 71), 0)
    student_key = draw_student_key(jax.random.fold_in(streams_of[5], 71), 0)
    head_mix = jnp.clip(jnp.exp(math.log(0.25) - 2.5257287 * jax.random.uniform(streams_of[4], (HEADS_T, HEADS_S), jnp.float32) ** level_of(streams_of[4], (HEADS_T, HEADS_S), ((0, 8),), -0.2, 0.2)), 0.02, 0.25)
    return dict(teacher_query=teacher_query, teacher_key=teacher_key, student_query=student_query, student_key=student_key, head_mix=head_mix)


HIGHEST = lax.Precision.HIGHEST


def one_image(query_t, key_t, query_s, key_s, head_mix):
    per_group = HEADS_T // N_HEAD
    block_rows = min(SEQ, 128)
    block_count = SEQ // block_rows
    all_query_t = query_t.astype(jnp.float32).reshape(SEQ, HEADS_T, HD_T)
    all_key_t = key_t.astype(jnp.float32).reshape(SEQ, HEADS_T, HD_T)
    all_query_s = query_s.astype(jnp.float32).reshape(SEQ, HEADS_S, HD_S)
    all_key_s = key_s.astype(jnp.float32).reshape(SEQ, HEADS_S, HD_S)
    mix_groups = head_mix.reshape(N_HEAD, per_group, HEADS_S)

    def visit(carry, index):
        key_grad, mix_grad = carry
        start = index * block_rows
        rows_t = lax.dynamic_slice_in_dim(all_query_t, start, block_rows, 0)
        rows_s = lax.dynamic_slice_in_dim(all_query_s, start, block_rows, 0)
        teacher = jnp.einsum("rhd,khd->hrk", rows_t, all_key_t, precision=HIGHEST) * HD_T ** -0.5
        student = jnp.einsum("rhd,khd->hrk", rows_s, all_key_s, precision=HIGHEST) * HD_S ** -0.5
        lifted = jnp.einsum("th,hrk->trk", head_mix, student, precision=HIGHEST)
        lse_t = jax.nn.logsumexp(teacher, axis=-1)
        lse_l = jax.nn.logsumexp(lifted, axis=-1)
        prob_t = jnp.exp(teacher - lse_t[..., None])
        prob_l = jnp.exp(lifted - lse_l[..., None])
        kl_rows = jnp.sum(prob_t * (teacher - lifted), axis=-1) - lse_t + lse_l
        excess = prob_l - prob_t
        mix_grad = mix_grad + jnp.einsum("trk,hrk->th", excess, student, precision=HIGHEST)
        grouped = jnp.einsum("gth,gtrk->ghrk", mix_groups, excess.reshape(N_HEAD, per_group, block_rows, SEQ), precision=HIGHEST)
        narrow = lax.optimization_barrier(grouped.astype(jnp.bfloat16))
        summed = jnp.sum(narrow.astype(jnp.float32), axis=0)
        query_grad = jnp.einsum("hrk,khd->rhd", summed, all_key_s, precision=HIGHEST).reshape(block_rows, HEADS_S * HD_S)
        key_grad = key_grad + jnp.einsum("hrk,rhd->khd", summed, rows_s, precision=HIGHEST)
        return (key_grad, mix_grad), (query_grad, jnp.sum(kl_rows, axis=-1))

    initial = (jnp.zeros((SEQ, HEADS_S, HD_S), jnp.float32), jnp.zeros((HEADS_T, HEADS_S), jnp.float32))
    (key_grad, mix_grad), (query_grads, losses) = lax.scan(visit, initial, jnp.arange(block_count, dtype=jnp.int32))
    return query_grads.reshape(SEQ, HEADS_S * HD_S), key_grad.reshape(SEQ, HEADS_S * HD_S), mix_grad, jnp.sum(losses, axis=0)


def reference(teacher_query, teacher_key, student_query, student_key, head_mix):
    weight = SEQ / HEADS_T
    factor = weight * HD_S ** -0.5
    outcomes = [one_image(teacher_query[image], teacher_key[image], student_query[image], student_key[image], head_mix) for image in range(IMAGES)]
    grad_query = jnp.stack([outcome[0] for outcome in outcomes]) * factor
    grad_key = jnp.stack([outcome[1] for outcome in outcomes]) * factor
    mix_total = jnp.sum(jnp.stack([outcome[2] for outcome in outcomes]), axis=0)
    loss_total = jnp.sum(jnp.stack([outcome[3] for outcome in outcomes]), axis=0)
    grad_mix = mix_total * (weight / (IMAGES * SEQ))
    head_loss = loss_total / (IMAGES * SEQ)
    return grad_query, grad_key, grad_mix, head_loss
```

```python
import functools

import jax
import jax.numpy as jnp
from jax import lax
from jax.experimental import pallas as pl
from jax.experimental.pallas import tpu as pltpu
from jax.sharding import PartitionSpec as P

HEADS_T = 24
HD_T = 128
HEADS_S = 8
HD_S = 64
MESH = pl.DeviceIdType.MESH
NT = (((1,), (1,)), ((), ()))
F32 = jnp.float32
VM = pltpu.VMEM
WHOLE = pl.BlockSpec(memory_space=pltpu.VMEM)
ANY = pl.BlockSpec(memory_space=pl.ANY)
SMEM = pl.BlockSpec(memory_space=pltpu.SMEM)
COLS = 2


def ring(axis, shift):
    n = lax.axis_size(axis)
    return lax.rem(lax.axis_index(axis) + (shift + n), n)


def remote(src, dst, send, recv, where):
    return pltpu.make_async_remote_copy(
        src_ref=src, dst_ref=dst, send_sem=send, recv_sem=recv,
        device_id=where, device_id_type=MESH)


def greet(places):
    barrier = pltpu.get_barrier_semaphore()
    for place in places:
        pl.semaphore_signal(barrier, inc=1, device_id=place, device_id_type=MESH)
    pl.semaphore_wait(barrier, len(places))


class Gather:
    def __init__(self, which, t_own, s_own, t_all, s_all, sems):
        self.which = which
        self.t_own, self.s_own, self.t_all, self.s_all = t_own, s_own, t_all, s_all
        self.ts, self.tr, self.zs, self.zr, self.ys, self.yr, self.local = sems
        self.n = lax.axis_size("seq")
        self.half = self.n // 2
        self.z = lax.axis_index("seq")
        g = lax.axis_index("head")
        self.rows = t_own.shape[0]
        self.ny = lax.axis_size("head") // COLS
        self.y = g // COLS
        self.x = lax.rem(g, COLS)
        self.sent = []

    def y_at(self, shift):
        return lax.rem(self.y + (shift + self.ny), self.ny)

    def y_place(self, shift):
        return {"head": self.y_at(shift) * COLS + self.x}

    def shard(self, way, s):
        return ring("seq", -s if way == 0 else s)

    def t_has(self, way, s, c):
        return s < self.half or (s == self.half and way == c)

    def s_has(self, way, s):
        return s < self.half or (s == self.half and way == self.which)

    def t_copy(self, way, s, c):
        step = self.rows // 2
        part = pl.ds(c * step, step)
        i = self.shard(way, s - 1)
        src = self.t_own.at[part] if s == 1 else self.t_all.at[i, part]
        return remote(src, self.t_all.at[i, part], self.ts.at[self.which, way, s, c],
                      self.tr.at[self.which, way, s, c],
                      {"seq": ring("seq", 1 if way == 0 else -1)})

    def s_piece(self):
        return self.s_own.at[:, pl.ds(pl.multiple_of(self.y * 128, 128), 128)]

    def s_copy(self, way, s):
        i = self.shard(way, s - 1)
        src = self.s_piece() if s == 1 else self.s_all.at[i, self.y]
        return remote(src, self.s_all.at[i, self.y], self.zs.at[self.which, way, s],
                      self.zr.at[self.which, way, s],
                      {"seq": ring("seq", 1 if way == 0 else -1)})

    def y_copy(self, way, s, hop):
        i = self.shard(way, s)
        to = 1
        q = self.y
        if hop == 1:
            to = -1
        if hop == 2:
            to = 1 if (s + way + self.which) % 2 == 0 else -1
            q = self.y_at(-to)
        src = self.s_piece() if s == 0 and hop < 2 else self.s_all.at[i, q]
        return remote(src, self.s_all.at[i, q], self.ys.at[self.which, way, s, hop],
                      self.yr.at[self.which, way, s, hop], self.y_place(to))

    def go(self, copy):
        copy.start()
        self.sent.append(copy)

    def ways(self, s):
        return [0] if s == 0 else [w for w in (0, 1) if self.s_has(w, s)]

    def begin(self):
        self.locals = [
            pltpu.make_async_copy(self.t_own, self.t_all.at[self.z], self.local.at[self.which, 0]),
        ]
        for q in range(self.ny):
            self.locals.append(pltpu.make_async_copy(
                self.s_own.at[:, q * 128:(q + 1) * 128], self.s_all.at[self.z, q], self.local.at[self.which, 1 + q]))
        for way in (0, 1):
            if self.s_has(way, 1):
                self.go(self.s_copy(way, 1))
        for way in (0, 1):
            for c in ((0, 1) if way == 0 else (1, 0)):
                if self.t_has(way, 1, c):
                    self.go(self.t_copy(way, 1, c))
        for c in self.locals:
            c.start()

    def s_step(self, s):
        for way in self.ways(s):
            self.s_copy(way, s).wait_recv()
            if self.s_has(way, s + 1):
                self.go(self.s_copy(way, s + 1))
            for hop in (0, 1):
                self.go(self.y_copy(way, s, hop))

    def y_step(self, s):
        for way in self.ways(s):
            self.y_copy(way, s, 0).wait_recv()
            self.y_copy(way, s, 1).wait_recv()
            self.go(self.y_copy(way, s, 2))

    def y_last(self, s):
        for way in self.ways(s):
            self.y_copy(way, s, 2).wait_recv()

    def t_step(self, s):
        for c in (0, 1):
            for way in ((0, 1) if c == 0 else (1, 0)):
                if self.t_has(way, s, c):
                    self.t_copy(way, s, c).wait_recv()
                    if self.t_has(way, s + 1, c):
                        self.go(self.t_copy(way, s + 1, c))

    def step(self, s):
        if s == 0:
            self.begin()
            return
        if s <= self.half:
            self.s_step(s)
        if 1 <= s - 1 <= self.half:
            self.y_step(s - 1)
        if 1 <= s - 2 <= self.half:
            self.y_last(s - 2)
        if s <= self.half:
            self.t_step(s)

    def finish(self):
        for c in self.locals:
            c.wait()
        for c in self.sent:
            c.wait_send()


def gather_kernel(tk, sk, tq, sq, tk_all, sk_all, tq_all, sq_all, *sems):
    n = lax.axis_size("seq")
    half = n // 2
    key = Gather(0, tk, sk, tk_all, sk_all, sems)
    query = Gather(1, tq, sq, tq_all, sq_all, sems)
    greet([{"seq": ring("seq", 1)}, {"seq": ring("seq", -1)}, key.y_place(1), key.y_place(-1)])
    for s in range(half):
        key.step(s)
    query.step(0)
    for s in range(half + 2 + 1):
        if s + half <= half + 2:
            key.step(s + half)
        query.step(s + 1)
    key.finish()
    query.finish()


def gather_sems(n):
    half = n // 2
    dma = pltpu.SemaphoreType.DMA
    return [dma((2, 2, half + 1, 2)), dma((2, 2, half + 1, 2)), dma((2, 2, half + 1)),
            dma((2, 2, half + 1)), dma((2, 2, half + 1, 3)), dma((2, 2, half + 1, 3)), dma((2, 5))]


def student_piece(ref, j, h):
    lanes = (h % 2) * HD_S
    return ref[j, h // 2, :, lanes:lanes + HD_S]


def row_logits(j, tq, sq, tk_all, sk_all, t_map, s_map):
    rows = tq.shape[0]
    lanes = pl.ds(pl.multiple_of(j * rows, rows), rows)
    for t in range(t_map.shape[0]):
        cols = slice(t * HD_T, (t + 1) * HD_T)
        t_map[t, :, lanes] = lax.dot_general(
            tq[:, cols], tk_all[j, :, cols], NT, preferred_element_type=F32) * HD_T ** -0.5
    for h in range(HEADS_S):
        s_map[h, :, lanes] = lax.dot_general(
            sq[:, h * HD_S:(h + 1) * HD_S], student_piece(sk_all, j, h), NT, preferred_element_type=F32)


RB = 16
WD = 128


def lift(mix, s):
    out = []
    for t in range(3):
        acc = mix[t][0] * s[0]
        for h in range(1, HEADS_S):
            acc = acc + mix[t][h] * s[h]
        out.append(acc)
    return out


def fold(mix, ex):
    return [mix[0][h] * ex[0] + mix[1][h] * ex[1] + mix[2][h] * ex[2] for h in range(HEADS_S)]


def mixes(mix, scale):
    return [[mix[t, h] * scale for h in range(HEADS_S)] for t in range(3)]


def row_piece(rb, mix_ref, t_map, s_map, l_map, et_map, el_map, back, stat, gm):
    heads = range(3)
    steps = t_map.shape[2] // WD
    rows = pl.ds(pl.multiple_of(rb * RB, RB), RB)
    m8 = mixes(mix_ref, HD_S ** -0.5)
    m1 = mixes(mix_ref, 1.0)

    def at(j):
        return pl.ds(pl.multiple_of(j * WD, WD), WD)

    def first(j, c):
        s = [s_map[h, rows, at(j)] for h in range(HEADS_S)]
        low = lift(m8, s)
        out = []
        for t in heads:
            l_map[t, :, at(j)] = low[t]
            out.append(jnp.maximum(c[t], t_map[t, rows, at(j)]))
        for t in heads:
            out.append(jnp.maximum(c[3 + t], low[t]))
        return tuple(out)

    floor = jnp.full((RB, WD), -1e30, F32)
    tops = lax.fori_loop(0, steps, first, (floor,) * 6)
    tops = [jnp.max(v, axis=-1, keepdims=True) for v in tops]
    wide = [jnp.broadcast_to(v, (RB, WD)) for v in tops]

    def second(j, c):
        out = list(c)
        for t in heads:
            a = t_map[t, rows, at(j)]
            b = l_map[t, :, at(j)]
            ea = jnp.exp(a - wide[t])
            eb = jnp.exp(b - wide[3 + t])
            et_map[t, :, at(j)] = ea
            el_map[t, :, at(j)] = eb
            out[t] = c[t] + ea
            out[3 + t] = c[3 + t] + eb
            out[6 + t] = c[6 + t] + ea * (a - b)
        return tuple(out)

    zero = jnp.zeros((RB, WD), F32)
    sums = lax.fori_loop(0, steps, second, (zero,) * 9)
    sums = [jnp.sum(v, axis=-1, keepdims=True) for v in sums]
    lane = lax.broadcasted_iota(jnp.int32, (RB, 128), 1)
    tile = jnp.zeros((RB, 128), F32)
    inv = [jnp.broadcast_to(1.0 / sums[k], (RB, WD)) for k in range(6)]
    for t in heads:
        lt = tops[t] + jnp.log(sums[t])
        ll = tops[3 + t] + jnp.log(sums[3 + t])
        kl = sums[6 + t] / sums[t] - lt + ll
        tile = jnp.where(lane == t, lt, tile)
        tile = jnp.where(lane == 3 + t, ll, tile)
        tile = jnp.where(lane == 8 + t, kl, tile)
    stat[rows, :] = tile

    def third(j, c):
        ex = [el_map[t, :, at(j)] * inv[3 + t] - et_map[t, :, at(j)] * inv[t] for t in heads]
        out = []
        for h in range(HEADS_S):
            s = s_map[h, rows, at(j)]
            for t in heads:
                p = ex[t] * s
                out.append(c[h * 3 + t] + (p[:8] + p[8:]))
            back[h, rows, at(j)] = (m1[0][h] * ex[0] + m1[1][h] * ex[1] + m1[2][h] * ex[2]).astype(jnp.bfloat16)
        return tuple(out)

    accs = lax.fori_loop(0, steps, third, (jnp.zeros((8, WD), F32),) * 24)
    for h in range(HEADS_S):
        for t in heads:
            gm[t * HEADS_S + h] += accs[h * 3 + t]


def row_stats(stat, gm, turned):
    a = stat[...].T
    turned[...] = jnp.zeros_like(turned)
    turned[0:24, :] = jnp.sum(gm[...], axis=1) * HD_S ** -0.5
    turned[24:32, :] = a[8:16, :]
    v = jnp.sum(turned[...].T, axis=0, keepdims=True)
    sub = lax.broadcasted_iota(jnp.int32, (8, 128), 0)
    return jnp.where(sub == 6, v, a[0:8, :])


def packed(v):
    return jnp.concatenate([v[:64], v[64:]], axis=1)


def row_grads(back, sk_all, out, scale):
    n, _, rows, _ = sk_all.shape
    for h in range(HEADS_S):
        lanes = (h % 2) * HD_S
        s = sk_all[:, h // 2, :, lanes:lanes + HD_S].reshape(n * rows, HD_S)
        r = jnp.dot(back[h], s, preferred_element_type=F32) * scale
        out[h] = packed(r)


def row_kernel(scale, mix, tq, sq, tk_all, sk_all, gq, small, t_map, s_map, l_map, et_map, el_map, back, stat, gm, turned):
    n = tk_all.shape[0]

    def logits(j, _):
        row_logits(j, tq, sq, tk_all, sk_all, t_map, s_map)
        return 0

    lax.fori_loop(0, n, logits, 0)
    gm[...] = jnp.zeros_like(gm)

    def piece(rb, _):
        row_piece(rb, mix, t_map, s_map, l_map, et_map, el_map, back, stat, gm)
        return 0

    lax.fori_loop(0, tq.shape[0] // RB, piece, 0)
    small[...] = row_stats(stat, gm, turned)
    row_grads(back, sk_all, gq, scale)


def row_scratch(n, rows):
    keys = n * rows
    return [VM((3, rows, keys), F32), VM((HEADS_S, rows, keys), F32), VM((3, RB, keys), F32),
            VM((3, RB, keys), F32), VM((3, RB, keys), F32), VM((HEADS_S, rows, keys), jnp.bfloat16),
            VM((rows, 128), F32), VM((24, 8, 128), F32), VM((128, 128), F32)]


def key_shard(j, mix_ref, tk, sk, tq_all, sq_all, lse, t_map, s_map, back):
    for t in range(3):
        cols = slice(t * HD_T, (t + 1) * HD_T)
        t_map[t] = lax.dot_general(
            tk[:, cols], tq_all[j, :, cols], NT, preferred_element_type=F32) * HD_T ** -0.5
    for h in range(HEADS_S):
        s_map[h] = lax.dot_general(
            sk[:, h * HD_S:(h + 1) * HD_S], student_piece(sq_all, j, h), NT, preferred_element_type=F32)
    m8 = mixes(mix_ref, HD_S ** -0.5)
    m1 = mixes(mix_ref, 1.0)
    wide = [jnp.broadcast_to(lse[j, k:k + 1, :], (RB, 128)) for k in range(6)]
    rows = tk.shape[0]
    lanes = pl.ds(pl.multiple_of(j * rows, rows), rows)

    def block(rb, _):
        r = pl.ds(pl.multiple_of(rb * RB, RB), RB)
        low = lift(m8, [s_map[h, r, :] for h in range(HEADS_S)])
        ex = [jnp.exp(low[t] - wide[3 + t]) - jnp.exp(t_map[t, r, :] - wide[t]) for t in range(3)]
        for h, v in enumerate(fold(m1, ex)):
            back[h, r, lanes] = v.astype(jnp.bfloat16)
        return 0

    lax.fori_loop(0, rows // RB, block, 0)


def key_kernel(scale, mix, tk, sk, tq_all, sq_all, lse, gk, t_map, s_map, back):
    def shard(j, _):
        key_shard(j, mix, tk, sk, tq_all, sq_all, lse, t_map, s_map, back)
        return 0

    lax.fori_loop(0, tq_all.shape[0], shard, 0)
    row_grads(back, sq_all, gk, scale)


def stats_kernel(small, out, send, recv, local):
    n = lax.axis_size("seq")
    z = lax.axis_index("seq")
    greet([{"seq": ring("seq", o)} for o in range(1, n)])
    own = pltpu.make_async_copy(small, out.at[z], local.at[0])
    own.start()
    copies = [remote(small, out.at[z], send.at[o], recv.at[o], {"seq": ring("seq", o)}) for o in range(1, n)]
    for c in copies:
        c.start()
    own.wait()
    for o in range(1, n):
        remote(small, out.at[ring("seq", -o)], send.at[o], recv.at[o], {"seq": ring("seq", o)}).wait_recv()
    for c in copies:
        c.wait_send()


def sums_kernel(gq, gk, stats, out_q, out_k, out_m, got, mine, tiles, send, recv, dsend, drecv):
    heads = lax.axis_size("head")
    dps = lax.axis_size("dp")
    g = lax.axis_index("head")
    total = stats[0]
    for j in range(1, stats.shape[0]):
        total = total + stats[j]
    mine[...] = total
    greet([{"head": ring("head", o)} for o in range(1, heads)] + [{"dp": ring("dp", o)} for o in range(1, dps)])
    copies = []
    for o in range(1, heads):
        to = ring("head", o)
        for k, ref in enumerate((gk, gq)):
            copies.append(remote(ref.at[to], got.at[k, o], send.at[k, o], recv.at[k, o], {"head": to}))
    for o in range(1, dps):
        copies.append(remote(mine, tiles.at[o], dsend.at[o], drecv.at[o], {"dp": ring("dp", o)}))
    for c in copies:
        c.start()
    for o in range(1, dps):
        remote(mine, tiles.at[o], dsend.at[o], drecv.at[o], {"dp": ring("dp", o)}).wait_recv()
        total = total + tiles[o]
    out_m[...] = total
    for k, (ref, out) in enumerate(((gk, out_k), (gq, out_q))):
        acc = ref[g]
        for o in range(1, heads):
            remote(ref.at[0], got.at[k, o], send.at[k, o], recv.at[k, o], {"head": ring("head", o)}).wait_recv()
            acc = acc + got[k, o]
        out[0:64, :] = acc[:, 0:64]
        out[64:128, :] = acc[:, 64:128]
    for c in copies:
        c.wait_send()


def body(teacher_query, teacher_key, student_query, student_key, head_mix):
    n = lax.axis_size("seq")
    tq, sq, tk, sk = teacher_query[0], student_query[0], teacher_key[0], student_key[0]
    rows = tq.shape[0]
    bf = jnp.bfloat16
    dma = pltpu.SemaphoreType.DMA
    t_shape = jax.ShapeDtypeStruct((n, *tq.shape), bf)
    s_shape = jax.ShapeDtypeStruct((n, sq.shape[1] // 128, rows, 128), bf)
    seq_len = rows * n
    weight = seq_len / HEADS_T
    factor = weight * HD_S ** -0.5
    images = lax.axis_size("dp")

    tk_all, sk_all, tq_all, sq_all = pl.pallas_call(
        gather_kernel, out_shape=(t_shape, s_shape, t_shape, s_shape),
        in_specs=[ANY] * 4, out_specs=[ANY] * 4, scratch_shapes=gather_sems(n), name="gather",
        compiler_params=pltpu.CompilerParams(collective_id=0, has_side_effects=True),
    )(tk, sk, tq, sq)

    grads = jax.ShapeDtypeStruct((HEADS_S, rows // 2, 128), F32)
    gq, small = pl.pallas_call(
        functools.partial(row_kernel, factor), out_shape=(grads, jax.ShapeDtypeStruct((8, 128), F32)),
        in_specs=[SMEM] + [WHOLE] * 4, out_specs=[WHOLE] * 2, scratch_shapes=row_scratch(n, rows), name="rows",
    )(head_mix, tq, sq, tk_all, sk_all)

    stats = pl.pallas_call(
        stats_kernel, out_shape=jax.ShapeDtypeStruct((n, 8, 128), F32),
        in_specs=[WHOLE], out_specs=WHOLE, scratch_shapes=[dma((n,)), dma((n,)), dma((1,))], name="stats",
        compiler_params=pltpu.CompilerParams(collective_id=1, has_side_effects=True),
    )(small)

    gk = pl.pallas_call(
        functools.partial(key_kernel, factor), out_shape=grads,
        in_specs=[SMEM] + [WHOLE] * 5, out_specs=WHOLE, name="keys",
        scratch_shapes=[VM((3, rows, rows), F32), VM((HEADS_S, rows, rows), F32), VM((HEADS_S, rows, n * rows), bf)],
    )(head_mix, tk, sk, tq_all, sq_all, stats)

    heads = lax.axis_size("head")
    out = jax.ShapeDtypeStruct((rows, HD_S), F32)
    out_q, out_k, out_m = pl.pallas_call(
        sums_kernel, out_shape=(out, out, jax.ShapeDtypeStruct((8, 128), F32)),
        in_specs=[WHOLE] * 3, out_specs=[WHOLE] * 3, name="sums",
        scratch_shapes=[VM((2, heads, rows // 2, 128), F32), VM((8, 128), F32), VM((images, 8, 128), F32),
                        dma((2, heads)), dma((2, heads)), dma((images,)), dma((images,))],
        compiler_params=pltpu.CompilerParams(collective_id=2, has_side_effects=True),
    )(gq, gk, stats)
    line = out_m[6]
    grad_mix = line[0:24].reshape(3, 8) * (weight / (images * seq_len))
    head_loss = line[24:27] / (images * seq_len)
    return out_q[None], out_k[None], grad_mix, head_loss


def solution(mesh):
    return jax.shard_map(
        body,
        mesh=mesh,
        in_specs=(
            P("dp", "seq", "head"),
            P("dp", "seq", "head"),
            P("dp", "seq", None),
            P("dp", "seq", None),
            P("head", None),
        ),
        out_specs=(P("dp", "seq", "head"), P("dp", "seq", "head"), P("head", None), P("head")),
        check_vma=False,
    )
```

```python
import functools
import itertools

import jax
import jax.numpy as jnp
from jax import lax
from jax.experimental import pallas as pl
from jax.experimental.pallas import tpu as pltpu
from jax.sharding import PartitionSpec as P

HEADS_T = 24
HD_T = 128
HEADS_S = 8
HD_S = 64
MESH = pl.DeviceIdType.MESH
NT = (((1,), (1,)), ((), ()))
F32 = jnp.float32
VM = pltpu.VMEM
WHOLE = pl.BlockSpec(memory_space=pltpu.VMEM)
ANY = pl.BlockSpec(memory_space=pl.ANY)
SMEM = pl.BlockSpec(memory_space=pltpu.SMEM)
COLS = 2
CHUNKS = 2
LAG = 3
GATE = 9
BEHIND = 1


def ring(axis, shift):
    n = lax.axis_size(axis)
    return lax.rem(lax.axis_index(axis) + (shift + n), n)


def remote(src, dst, send, recv, where):
    return pltpu.make_async_remote_copy(
        src_ref=src, dst_ref=dst, send_sem=send, recv_sem=recv,
        device_id=where, device_id_type=MESH)


def greet(places, while_waiting):
    barrier = pltpu.get_barrier_semaphore()
    for place in places:
        pl.semaphore_signal(barrier, inc=1, device_id=place, device_id_type=MESH)
    while_waiting()
    pl.semaphore_wait(barrier, len(places))


class Gather:
    def __init__(self, which, t_own, s_own, t_all, s_all, sems):
        self.which = which
        self.t_own, self.s_own, self.t_all, self.s_all = t_own, s_own, t_all, s_all
        self.ts, self.tr, self.zs, self.zr, self.ys, self.yr, self.local = sems
        self.n = lax.axis_size("seq")
        self.half = self.n // 2
        g = lax.axis_index("head")
        self.rows = t_own.shape[0]
        self.ny = lax.axis_size("head") // COLS
        self.y = g // COLS
        self.x = lax.rem(g, COLS)
        self.sent = []
        self.locals = [
            pltpu.make_async_copy(self.t_own, self.t_all.at[0], self.local.at[self.which, 0]),
            pltpu.make_async_copy(self.s_own, self.s_all.at[0], self.local.at[self.which, 1]),
        ]

    def y_at(self, shift):
        return lax.rem(self.y + (shift + self.ny), self.ny)

    def y_place(self, shift):
        return {"head": self.y_at(shift) * COLS + self.x}

    def slot(self, way, s):
        return 0 if s == 0 else 2 * s - 1 if way == 0 or s == self.half else 2 * s

    def t_has(self, way, s, c):
        return s < self.half or (s == self.half and way == c // (CHUNKS // 2))

    def s_has(self, way, s):
        return s < self.half or (s == self.half and way == self.which)

    def t_copy(self, way, s, c):
        step = self.rows // CHUNKS
        part = pl.ds(c * step, step)
        src = self.t_own.at[part] if s == 1 else self.t_all.at[self.slot(way, s - 1), part]
        return remote(src, self.t_all.at[self.slot(way, s), part], self.ts.at[self.which, way, s, c],
                      self.tr.at[self.which, way, s, c],
                      {"seq": ring("seq", 1 if way == 0 else -1)})

    def quarter(self, ref, q):
        return ref.at[:, pl.ds(pl.multiple_of(q * 128, 128), 128)]

    def s_copy(self, way, s):
        src = self.quarter(self.s_own, self.y) if s == 1 else self.quarter(self.s_all.at[self.slot(way, s - 1)], self.y)
        return remote(src, self.quarter(self.s_all.at[self.slot(way, s)], self.y), self.zs.at[self.which, way, s],
                      self.zr.at[self.which, way, s],
                      {"seq": ring("seq", 1 if way == 0 else -1)})

    def y_copy(self, way, s, hop):
        ref = self.quarter(self.s_all.at[self.slot(way, s)], self.y)
        return remote(ref, ref, self.ys.at[self.which, way, s, hop], self.yr.at[self.which, way, s, hop],
                      self.y_place((1, -1, 2)[hop]))

    def go(self, copy):
        copy.start()
        self.sent.append(copy)

    def ways(self, s):
        return [0] if s == 0 else [w for w in (0, 1) if self.s_has(w, s)]

    def begin(self):
        for way in (0, 1):
            if self.s_has(way, 1):
                self.go(self.s_copy(way, 1))
        for c in range(CHUNKS):
            for way in (0, 1):
                if self.t_has(way, 1, c):
                    self.go(self.t_copy(way, 1, c))

    def s_step(self, s):
        for way in self.ways(s):
            self.s_copy(way, s).wait_recv()
            if self.s_has(way, s + 1):
                self.go(self.s_copy(way, s + 1))
            for hop in range(3):
                self.go(self.y_copy(way, s, hop))

    def y_step(self, s):
        for way in self.ways(s):
            for hop in range(3):
                self.y_copy(way, s, hop).wait_recv()

    def t_step(self, s, c):
        for way in (0, 1):
            if self.t_has(way, s, c):
                self.t_copy(way, s, c).wait_recv()
                if self.t_has(way, s + 1, c):
                    self.go(self.t_copy(way, s + 1, c))

    def ticks(self, s):
        h = self.half
        if 1 <= s <= h:
            yield lambda: self.s_step(s), 0
            for c in range(CHUNKS):
                yield functools.partial(self.t_step, s, c), 0
        for a in range(1, h + 1):
            if min(a + BEHIND, h + 1) == s:
                yield functools.partial(self.y_step, a), a

    def own_here(self):
        for c in self.locals:
            c.wait()

    def finish(self):
        for c in self.sent:
            c.wait_send()


def gather_sems(n):
    half = n // 2
    dma = pltpu.SemaphoreType.DMA
    return [dma((2, 2, half + 1, CHUNKS)), dma((2, 2, half + 1, CHUNKS)), dma((2, 2, half + 1)),
            dma((2, 2, half + 1)), dma((2, 2, half + 1, 3)), dma((2, 2, half + 1, 3)), dma((2, 2))]


RB = 16
LOG = HD_T ** -0.5


def mix_row(mix, t):
    group = lax.broadcasted_iota(jnp.int32, (1, HEADS_S * HD_S), 1) // HD_S
    row = jnp.full(group.shape, mix[t, 0], F32)
    for h in range(1, HEADS_S):
        row = jnp.where(group == h, mix[t, h], row)
    return row


def weigh(mix, own, out):
    wide = own[...].astype(F32)
    rows = own.shape[0]
    for t in range(3):
        v = wide * (mix_row(mix, t) * HD_S ** -0.5)
        high = v.astype(jnp.bfloat16)
        out[0, t * rows:(t + 1) * rows, :] = high
        out[1, t * rows:(t + 1) * rows, :] = (v - high.astype(F32)).astype(jnp.bfloat16)


def logits(lo, cnt, t_own, weighed, t_all, s_all, t_map, l_map, at):
    rows = t_own.shape[0]
    lanes = slice(at * rows, (at + cnt) * rows)
    for t in range(3):
        cols = slice(t * HD_T, (t + 1) * HD_T)
        other = t_all[lo:lo + cnt, :, cols].reshape(cnt * rows, HD_T)
        t_map[t, :, lanes] = lax.dot_general(t_own[:, cols], other, NT, preferred_element_type=F32) * LOG
    other = s_all[lo:lo + cnt].reshape(cnt * rows, HEADS_S * HD_S)
    low = lax.dot_general(weighed[0], other, NT, preferred_element_type=F32)
    low = low + lax.dot_general(weighed[1], other, NT, preferred_element_type=F32)
    for t in range(3):
        l_map[t, :, lanes] = low[t * rows:(t + 1) * rows]


def online(lo, cnt, t_map, l_map, top, tot, div):
    rows = t_map.shape[1]

    def block(rb, _):
        r = pl.ds(pl.multiple_of(rb * RB, RB), RB)
        for t in range(3):
            a = [t_map[t, r, (lo + i) * rows:(lo + i + 1) * rows] for i in range(cnt)]
            b = [l_map[t, r, (lo + i) * rows:(lo + i + 1) * rows] for i in range(cnt)]
            new = functools.reduce(jnp.maximum, a, top[t, r, :])
            fade = jnp.exp(top[t, r, :] - new)
            ea = [jnp.exp(v - new) for v in a]
            top[t, r, :] = new
            tot[t, r, :] = tot[t, r, :] * fade + sum(ea[1:], ea[0])
            terms = [e * (u - v) for e, u, v in zip(ea, a, b)]
            div[t, r, :] = div[t, r, :] * fade + sum(terms[1:], terms[0])
            new = functools.reduce(jnp.maximum, b, top[3 + t, r, :])
            fade = jnp.exp(top[3 + t, r, :] - new)
            eb = [jnp.exp(v - new) for v in b]
            top[3 + t, r, :] = new
            tot[3 + t, r, :] = tot[3 + t, r, :] * fade + sum(eb[1:], eb[0])
        return 0

    lax.fori_loop(0, rows // RB, block, 0)


def settle(top, tot, div, stat):
    shape = stat.shape
    lane = lax.broadcasted_iota(jnp.int32, shape, 1)
    tile = jnp.zeros(shape, F32)
    lse, fade, tots = [], [], []
    for k in range(6):
        m = top[k]
        best = jnp.max(m, axis=-1, keepdims=True)
        f = jnp.exp(m - best)
        s = jnp.sum(tot[k] * f, axis=-1, keepdims=True)
        lse.append(best + jnp.log(s))
        fade.append(f)
        tots.append(s)
    for k in range(6):
        wide = jnp.broadcast_to(lse[k], shape)
        top[k] = wide
        tile = jnp.where(lane == k, wide, tile)
    for t in range(3):
        d = jnp.sum(div[t] * fade[t], axis=-1, keepdims=True) / tots[t] - lse[t] + lse[3 + t]
        tile = jnp.where(lane == 8 + t, d, tile)
    stat[...] = tile
    return stat[...].T


def fold(weights, ex):
    return [weights[0][h] * ex[0] + weights[1][h] * ex[1] + weights[2][h] * ex[2] for h in range(HEADS_S)]


def excess(lo, cnt, mix, t_map, l_map, lse_of, ex, back):
    rows = t_map.shape[1]
    weights = [[mix[t, h] for h in range(HEADS_S)] for t in range(3)]

    def block(rb, _):
        r = pl.ds(pl.multiple_of(rb * RB, RB), RB)
        for i in range(cnt):
            lanes = slice((lo + i) * rows, (lo + i + 1) * rows)
            here = slice(i * rows, (i + 1) * rows)
            v = [jnp.exp(l_map[t, r, lanes] - lse_of(3 + t, i, r)) - jnp.exp(t_map[t, r, lanes] - lse_of(t, i, r))
                 for t in range(3)]
            for h, b in enumerate(fold(weights, v)):
                back[h, r, here] = b.astype(jnp.bfloat16)
            if ex is not None:
                for t in range(3):
                    ex[pl.ds(pl.multiple_of(t * rows + rb * RB, RB), RB), here] = v[t].astype(jnp.bfloat16)
        return 0

    lax.fori_loop(0, rows // RB, block, 0)


def heads_up(lo, cnt, back, s_all, acc, first):
    rows = s_all.shape[1]
    for h in range(HEADS_S):
        other = s_all[lo:lo + cnt, :, h * HD_S:(h + 1) * HD_S].reshape(cnt * rows, HD_S)
        v = jnp.dot(back[h, :, 0:cnt * rows], other, preferred_element_type=F32)
        acc[h] = v if first else acc[h] + v


def gather_up(lo, cnt, ex, s_all, acc, first):
    rows = s_all.shape[1]
    v = jnp.dot(ex[:, 0:cnt * rows], s_all[lo:lo + cnt].reshape(cnt * rows, HEADS_S * HD_S), preferred_element_type=F32)
    acc[...] = v if first else acc[...] + v


def combine(acc, factor, out):
    for h in range(HEADS_S):
        out[h] = (acc[h] * factor).T


def mix_sums(acc, sq, turned, out):
    rows = sq.shape[0]
    wide = sq[...].astype(F32)
    sub = lax.broadcasted_iota(jnp.int32, (8, 128), 0)
    lane = lax.broadcasted_iota(jnp.int32, (8, 128), 1)
    lines = [jnp.sum(acc[t * rows:(t + 1) * rows, :] * wide, axis=0, keepdims=True) for t in range(3)]
    tile = jnp.zeros((8, 128), F32)
    for t in range(3):
        own = jnp.sum(turned[8 + t:9 + t, :], axis=-1, keepdims=True)
        tile = jnp.where((sub == 3) & (lane == t), own, tile)
    for q in range(4):
        v = jnp.zeros((8, 128), F32)
        for t in range(3):
            v = jnp.where(sub == t, lines[t][:, q * 128:(q + 1) * 128], v)
        for k in range(2):
            own = jnp.sum(jnp.where(lane // HD_S == k, v, 0.0), axis=-1, keepdims=True) * HD_S ** -0.5
            tile = jnp.where((lane == 2 * q + k) & (sub < 3), own, tile)
    out[...] = tile


class Plan:
    def __init__(self, blocks, key_block, lse_in):
        self.soon, self.later = [], []
        self.blocks, self.key_block, self.lse_in = blocks, key_block, lse_in
        self.units, self.done, self.since = 0, 0, None

    def sent(self, lse_out):
        lse_out()
        self.since = 0

    def have(self, all_of_it):
        self.units = 2 * self.blocks if all_of_it else self.units + 1

    def key_side(self):
        if self.done == self.blocks or self.units < min(2 * self.done + 2, 2 * self.blocks):
            return False
        if self.lse_in:
            self.lse_in()
            self.lse_in = None
        self.key_block(4 * self.done, 4)
        self.done += 1
        return True

    def step(self):
        if self.since is not None:
            self.since += 1
        if self.soon:
            self.soon.pop(0)()
        elif self.later:
            self.later.pop(0)()
        elif self.since is not None and self.since >= GATE:
            self.key_side()

    def drain(self):
        while self.soon or self.later:
            (self.soon or self.later).pop(0)()
        while self.key_side():
            pass


def main_kernel(factor, mix, tk, sk, tq, sq, got, tiles,
                tk_all, sk_all, tq_all, sq_all, mq, mk, t_map, l_map, t_map2, l_map2, top, tot, div, ex, back, x_acc, q_acc, k_acc, stat,
                own_lse, lse_all, own_sum, sums_all, dp_sum, gq, gk, *sems):
    n = lax.axis_size("seq")
    heads, dps = lax.axis_size("head"), lax.axis_size("dp")
    z, g, d = lax.axis_index("seq"), lax.axis_index("head"), lax.axis_index("dp")
    half = n // 2
    lsend, lrecv, msend, mrecv, dsend, drecv, rsend, rrecv, own_sems = sems[7:]
    key = Gather(0, tk, sk, tk_all, sk_all, sems[:7])
    query = Gather(1, tq, sq, tq_all, sq_all, sems[:7])
    held = {}
    sent = []

    def unit(s):
        return (0, 1) if s == 0 else (2 * s - 1, 1 if s == half else 2)

    def row_unit(s):
        lo, cnt = unit(s)
        logits(lo, cnt, tq, mq, tk_all, sk_all, t_map, l_map, lo)
        online(lo, cnt, t_map, l_map, top, tot, div)

    def row_block(b):
        excess(4 * b, 4, mix, t_map, l_map, lambda k, i, r: top[k, r, :], ex, back)
        heads_up(4 * b, 4, back, sk_all, q_acc, b == 0)
        gather_up(4 * b, 4, ex, sk_all, x_acc, b == 0)

    def key_logits(s):
        lo, cnt = unit(s)
        logits(lo, cnt, tk, mk, tq_all, sq_all, t_map2, l_map2, lo)

    def key_block(lo, cnt):
        wide = [[jnp.broadcast_to(lse_all[lo + i, k:k + 1, :], (RB, 128)) for k in range(6)] for i in range(cnt)]
        excess(lo, cnt, mix, t_map2, l_map2, lambda k, i, r: wide[i][k], None, back)
        heads_up(lo, cnt, back, sq_all, k_acc, lo == 0)

    def first():
        for c in key.locals + query.locals:
            c.start()
        weigh(mix, sq, mq)
        weigh(mix, sk, mk)
        top[...] = jnp.full_like(top, -1e30)
        tot[...] = jnp.zeros_like(tot)
        div[...] = jnp.zeros_like(div)
        key.own_here()
        query.own_here()
        row_unit(0)

    def spread(copies):
        for c in copies:
            c.start()
            sent.append(c)

    def lse_copy(o):
        place = 2 * o - 1 if o <= half else 2 * (n - o)
        return remote(own_lse, lse_all.at[place], lsend.at[o], lrecv.at[o], {"seq": ring("seq", o)})

    def sum_copy(o, at):
        return remote(own_sum, sums_all.at[at], msend.at[o], mrecv.at[o], {"seq": ring("seq", o)})

    def dp_copy(o, at):
        return remote(dp_sum, tiles.at[at], dsend.at[o], drecv.at[o], {"dp": ring("dp", o)})

    def slice_copy(k, ref, o):
        to = ring("head", o)
        return remote(ref.at[to], got.at[k, o], rsend.at[k, o], rrecv.at[k, o], {"head": to})

    def keep(copy):
        copy.start()
        return copy

    def lse_ready():
        held["turned"] = settle(top, tot, div, stat)
        own_lse[...] = held["turned"][0:8, :]

    def lse_out():
        held["lse"] = keep(pltpu.make_async_copy(own_lse, lse_all.at[0], own_sems.at[0]))
        spread(lse_copy(o) for o in range(1, n))

    def row_end():
        mix_sums(x_acc, sq, held["turned"], own_sum)
        combine(q_acc, factor, gq)

    def row_out():
        held["sum"] = keep(pltpu.make_async_copy(own_sum, sums_all.at[z], own_sems.at[1]))
        held["gq"] = keep(pltpu.make_async_copy(gq.at[g], got.at[1, 0], own_sems.at[2]))
        spread(sum_copy(o, z) for o in range(1, n))
        spread(slice_copy(1, gq, o) for o in range(1, heads))

    def lse_in():
        held["lse"].wait()
        for o in range(1, n):
            lse_copy(o).wait_recv()

    def total_of_images():
        held["sum"].wait()
        for o in range(1, n):
            sum_copy(o, z).wait_recv()
        total = sums_all[0]
        for j in range(1, n):
            total = total + sums_all[j]
        dp_sum[...] = total

    def dp_out():
        held["dp"] = keep(pltpu.make_async_copy(dp_sum, tiles.at[d], own_sems.at[1]))
        spread(dp_copy(o, d) for o in range(1, dps))

    greet([{"seq": ring("seq", o)} for o in (1, n - 1)] + [{"head": ring("head", o)} for o in range(1, heads)]
          + [{"dp": ring("dp", o)} for o in range(1, dps)], first)
    key.begin()
    plan = Plan(n // 4, key_block, lse_in)
    plan.later.append(functools.partial(key_logits, 0))
    def arrived(k, q):
        if k:
            plan.soon.append(functools.partial(row_unit, k))
            if k == half:
                plan.soon += [lse_ready, lambda: plan.sent(lse_out)]
                plan.soon += [functools.partial(row_block, b) for b in range(n // 4)]
                plan.soon += [row_end, lambda: None, row_out]
        if q:
            plan.later.append(functools.partial(key_logits, q))
            plan.later.append(functools.partial(plan.have, q == half))

    for i in range(1, half + 3 + LAG):
        if i == LAG:
            query.begin()
        for k, q in itertools.zip_longest(key.ticks(i), query.ticks(i - LAG)):
            if k:
                k[0]()
                arrived(k[1], 0)
                plan.step()
            if q:
                q[0]()
                arrived(0, q[1])
                plan.step()
    plan.drain()
    total_of_images()
    combine(k_acc, factor, gk)
    dp_out()
    key.finish()
    query.finish()
    held["gk"] = keep(pltpu.make_async_copy(gk.at[g], got.at[0, 0], own_sems.at[0]))
    spread(slice_copy(0, gk, o) for o in range(1, heads))
    for name in ("gq", "dp", "gk"):
        held[name].wait()
    for o in range(1, heads):
        slice_copy(1, gq, o).wait_recv()
    for o in range(1, dps):
        dp_copy(o, d).wait_recv()
    for o in range(1, heads):
        slice_copy(0, gk, o).wait_recv()
    for c in sent:
        c.wait_send()


def last_kernel(scale_mix, scale_loss, got, tiles, out_q, out_k, out_mix, out_loss):
    for k, out in enumerate((out_k, out_q)):
        acc = got[k, 0]
        for o in range(1, got.shape[1]):
            acc = acc + got[k, o]
        out[...] = acc
    total = tiles[0]
    for j in range(1, tiles.shape[0]):
        total = total + tiles[j]
    out_mix[...] = total[0:3, 0:8] * scale_mix
    out_loss[...] = total[3, 0:3] * scale_loss


def body(teacher_query, teacher_key, student_query, student_key, head_mix):
    n = lax.axis_size("seq")
    tq, sq, tk, sk = teacher_query[0], student_query[0], teacher_key[0], student_key[0]
    rows = tq.shape[0]
    bf = jnp.bfloat16
    dma = pltpu.SemaphoreType.DMA
    seq_len = rows * n
    weight = seq_len / HEADS_T
    factor = weight * HD_S ** -0.5
    images = lax.axis_size("dp")
    heads = lax.axis_size("head")
    width = HEADS_S * HD_S
    t_all, s_all = VM((n, *tq.shape), bf), VM((n, *sq.shape), bf)
    weighed = VM((2, 3 * rows, width), bf)
    got, tiles = pl.pallas_call(
        functools.partial(main_kernel, factor),
        out_shape=(jax.ShapeDtypeStruct((2, heads, HD_S, rows), F32), jax.ShapeDtypeStruct((images, 8, 128), F32)),
        in_specs=[SMEM] + [WHOLE] * 4, out_specs=[ANY] * 2, name="main",
        scratch_shapes=[
            t_all, s_all, t_all, s_all, weighed, weighed,
            *[VM((3, rows, n * rows), F32)] * 4,
            VM((6, rows, 128), F32), VM((6, rows, 128), F32), VM((3, rows, 128), F32),
            VM((3 * rows, 4 * rows), bf), VM((HEADS_S, rows, 4 * rows), bf), VM((3 * rows, width), F32),
            VM((HEADS_S, rows, HD_S), F32), VM((HEADS_S, rows, HD_S), F32),
            VM((rows, 128), F32), VM((8, 128), F32), VM((n, 8, 128), F32),
            VM((8, 128), F32), VM((n, 8, 128), F32), VM((8, 128), F32),
            VM((HEADS_S, HD_S, rows), F32), VM((HEADS_S, HD_S, rows), F32),
        ] + gather_sems(n) + [dma((n,)), dma((n,)), dma((n,)), dma((n,)), dma((images,)), dma((images,)),
                              dma((2, heads)), dma((2, heads)), dma((3,))],
        compiler_params=pltpu.CompilerParams(collective_id=0, has_side_effects=True),
    )(head_mix, tk, sk, tq, sq)
    out = jax.ShapeDtypeStruct((HD_S, rows), F32)
    out_q, out_k, out_mix, out_loss = pl.pallas_call(
        functools.partial(last_kernel, weight / (images * seq_len), 1.0 / (images * seq_len)),
        out_shape=(out, out, jax.ShapeDtypeStruct((3, 8), F32), jax.ShapeDtypeStruct((3,), F32)),
        in_specs=[WHOLE] * 2, out_specs=[WHOLE] * 4, name="last",
    )(got, tiles)
    return out_q.T[None], out_k.T[None], out_mix, out_loss


def solution(mesh):
    return jax.shard_map(
        body,
        mesh=mesh,
        in_specs=(
            P("dp", "seq", "head"),
            P("dp", "seq", "head"),
            P("dp", "seq", None),
            P("dp", "seq", None),
            P("head", None),
        ),
        out_specs=(P("dp", "seq", "head"), P("dp", "seq", "head"), P("head", None), P("head")),
        check_vma=False,
    )
```
